32 devices in a mesh: dp: 8 (over y, x, core), mp: 4 (over z).
Axes of the slice: x: 2, y: 2, z: 4, core: 2. Of those that a mesh axis runs over, the one named last changes fastest.
Arguments:
- buffer: bfloat16 [65536, 256], P(('dp', 'mp')), may hold values from -24 to 24, as said below
- owner: int32 [32768, 1], P(('dp', 'mp')), may hold values from 0 to 31; in each aligned block of 1024 rows (0 to 1023, 1024 to 2047, ...) at most 128 rows name the same one
- local_row: int32 [32768], P(('dp', 'mp')), may hold values from 0 to 2047
- q_in: bfloat16 [2, 130, 256], replicated, may hold values from -0.5 to 0.5
- q_mid: bfloat16 [2, 256, 256], replicated, may hold values from -0.5 to 0.5
- q_out: bfloat16 [2, 256], replicated, may hold values from -0.5 to 0.5
- v_in: bfloat16 [124, 256], replicated, may hold values from -0.5 to 0.5
- v_mid: bfloat16 [256, 256], replicated, may hold values from -0.5 to 0.5
- v_out: bfloat16 [256], replicated, may hold values from -0.5 to 0.5
Outputs:
- q_values: float32 [2, 32768], P(None, ('dp', 'mp'))
- values: float32 [2, 32768], P(None, ('dp', 'mp'))
- targets: float32 [32768], P(('dp', 'mp'))
- q_loss: float32 [32768], P(('dp', 'mp'))
- value_loss: float32 [32768], P(('dp', 'mp'))
The draws below stay inside these ranges and needn't reach their ends.
Inputs may be any that keep to these rules, and one draw needn't show every extreme that they name: Owner o is the replay owner at position o of the devices in dp+mp order. In the rows of one reader no owner is named more than 128 times, a bound that some block reaches. `buffer`: action values lie in -1 to 1 and discounts in 0 to 0.99.
All inputs are finite; a program needn't handle non-finite values.
Results may differ from the reference program's by a relative error of at most 0.005.
Values may be sent and summed in bfloat16 or wider, within the bound.
A program may use at most 64 MiB of HBM per device.

```python
import math
import jax
import jax.numpy as jnp
import numpy as np
from jax import lax

S = 124
A = 6
H = 256
ROWS_DEV = 2048
B_DEV = 1024
CAP = 128
ROWS = 65536
BATCH = 32768
DEVICES = 32


def draw_buffer(key, part):
    keys = jax.random.split(jax.random.fold_in(key, 17), 5)
    states = jnp.clip(jax.random.normal(keys[0], (ROWS, S), jnp.float32), -6.0, 6.0)
    actions = jax.random.uniform(keys[1], (ROWS, A), jnp.float32, -1.0, 1.0)
    nexts = jnp.clip(jax.random.normal(keys[2], (ROWS, S), jnp.float32), -6.0, 6.0)
    reward = jnp.clip(jax.random.normal(keys[3], (ROWS, 1), jnp.float32), -6.0, 6.0)
    discount = jax.random.uniform(keys[4], (ROWS, 1), jnp.float32, 0.0, 0.99)
    return jnp.concatenate([states, actions, nexts, reward, discount], axis=1).astype(jnp.bfloat16)


def with_ends(result, key, low, largest):
    dims = result.shape
    place = [jax.random.randint(jax.random.fold_in(key, axis), (), 0, dims[axis]) for axis in range(len(dims))]
    result = result.at[tuple(place)].set(low)
    longest = dims.index(max(dims))
    place[longest] = (place[longest] + 1) % dims[longest]
    return result.at[tuple(place)].set(largest)


def assign_block(stream_key, own, number, rows, count, top, bound, skew):
    order = jax.random.permutation(stream_key, count)
    heavy_load, common = shares(count, rows * top, bound, skew, True), shares(count, rows * top, bound, skew, False)
    places = jnp.arange(count)

    def named(sizes, rotation):
        used = int((sizes > 0).sum())
        fixed = max(1, used // 4)
        moved = fixed + (places - fixed + rotation * (used - fixed)) % max(1, count - fixed)
        return jnp.zeros((count,), jnp.int32).at[order[jnp.where(places < fixed, places, moved)]].set(jnp.asarray(sizes, jnp.int32))

    sizes = jnp.where(number % 4 == 0, named(heavy_load, number // 4), named(common, number - number // 4 - 1))
    mixed = jax.random.permutation(jax.random.fold_in(own, 3), count)
    donor, taker = mixed[0:count // 2 * 2:2], mixed[1:count // 2 * 2:2]
    room = jnp.minimum(sizes[donor] - 1, bound - sizes[taker]) // 2
    room = jnp.where((donor == order[0]) | (taker == order[0]) | (sizes[taker] == 0), 0, jnp.maximum(room, 0))
    moved = jax.random.randint(jax.random.fold_in(own, 4), (count // 2,), 0, 1 << 20) % (room + 1)
    sizes = sizes.at[donor].add(-moved).at[taker].add(moved)
    members = jnp.searchsorted(jnp.cumsum(sizes), jnp.arange(rows * top), side="right").astype(jnp.int32)
    listing = members.reshape(top, rows).T
    listing = listing[jax.random.permutation(jax.random.fold_in(own, 1), rows)]
    rotation = jax.random.randint(jax.random.fold_in(own, 2), (rows, 1), 0, top)
    return jnp.take_along_axis(listing, (jnp.arange(top)[None, :] + rotation) % top, axis=1)


def shares(number_of, total, reach, skew, full):
    weights = [(1 << 20) // math.isqrt(grade ** skew) + 1 for grade in range(1, number_of + 1)]
    largest = reach if full else min(reach, max(-(-total // number_of), total * weights[0] // sum(weights)))
    least = 1 if total - largest >= number_of - 1 else 0
    holding, surplus = [largest] + [least] * (number_of - 1), total - largest - least * (number_of - 1)
    while surplus > 0:
        candidates = [i for i in range(1, number_of) if holding[i] < largest] or [i for i in range(1, number_of) if holding[i] < reach]
        whole, remaining = sum([weights[i] for i in candidates]), surplus
        for i in candidates:
            more = min(reach - holding[i], max(1, remaining * weights[i] // whole), surplus)
            holding[i] = holding[i] + more
            surplus = surplus - more
    return np.array(holding)


def scatter_about(key, extent, spread, bound, kind=jnp.bfloat16):
    drawn = spread * jax.random.normal(key, extent, jnp.float32)
    return jnp.clip(drawn, min=-bound, max=bound).astype(kind)


def setup_inputs(seed: int = 0) -> dict:
    splits = jax.random.split(jax.random.key(seed), 10)
    buffer = draw_buffer(jax.random.fold_in(splits[9], 71), 0)
    owner_keys = jax.random.split(jax.random.fold_in(splits[1], 1), BATCH // B_DEV)
    owner_turns = jax.random.permutation(jax.random.fold_in(splits[1], 3), BATCH // B_DEV)
    owner = jax.vmap(lambda own, number: assign_block(jax.random.fold_in(splits[1], 2), own, number, B_DEV, DEVICES, 1, CAP, 2))(owner_keys, owner_turns).reshape((BATCH, 1))
    local_row = with_ends(jax.random.randint(splits[2], (BATCH,), 0, ROWS_DEV), jax.random.fold_in(splits[2], 1), 0, ROWS_DEV - 1).astype(jnp.int32)
    q_in = scatter_about(splits[3], (2, S + A, H), (S + A) ** -0.5, 0.5)
    q_mid = scatter_about(splits[4], (2, H, H), (H // 2) ** -0.5, 0.5)
    q_out = scatter_about(splits[5], (2, H), (H // 2) ** -0.5, 0.5)
    v_in = scatter_about(splits[6], (S, H), S ** -0.5, 0.5)
    v_mid = scatter_about(splits[7], (H, H), (H // 2) ** -0.5, 0.5)
    v_out = scatter_about(splits[8], (H,), (H // 2) ** -0.5, 0.5)
    return dict(buffer=buffer, owner=owner, local_row=local_row, q_in=q_in, q_mid=q_mid, q_out=q_out, v_in=v_in, v_mid=v_mid, v_out=v_out)


def layer_two(first, mid, out):
    hidden = jnp.maximum(jnp.dot(first, mid, preferred_element_type=jnp.float32), 0.0)
    return jnp.dot(hidden, out.astype(jnp.float32), precision=lax.Precision.HIGHEST)


def critic_block(rows, q_in, q_mid, q_out, v_in, v_mid, v_out):
    pair = rows[:, :S + A]
    state = rows[:, :S]
    nexts = rows[:, S + A:2 * S + A]
    reward = rows[:, 2 * S + A].astype(jnp.float32)
    discount = rows[:, 2 * S + A + 1].astype(jnp.float32)
    qs = []
    for head in range(2):
        first = jnp.maximum(jnp.dot(pair, q_in[head], preferred_element_type=jnp.float32), 0.0).astype(jnp.bfloat16)
        qs.append(layer_two(first, q_mid[head], q_out[head]))
    both = jnp.concatenate([state, nexts], axis=0)
    vfirst = jnp.maximum(jnp.dot(both, v_in, preferred_element_type=jnp.float32), 0.0).astype(jnp.bfloat16)
    vall = layer_two(vfirst, v_mid, v_out)
    batch = state.shape[0]
    value_now = vall[:batch]
    value_next = vall[batch:]
    targets = reward + discount * value_next
    return qs[0], qs[1], value_now, value_next, targets


def reference(buffer, owner, local_row, q_in, q_mid, q_out, v_in, v_mid, v_out):
    index = (owner[:, 0] * ROWS_DEV + local_row).astype(jnp.int32)
    blocks = index.reshape(-1, B_DEV)

    def one_block(picks):
        rows = jnp.take(buffer, picks, axis=0)
        return critic_block(rows, q_in, q_mid, q_out, v_in, v_mid, v_out)

    results = lax.map(one_block, blocks)
    q_first, q_second, value_now, value_next, targets = [r.reshape(-1) for r in results]
    q_loss = (q_first - targets) ** 2 + (q_second - targets) ** 2
    gap = jnp.minimum(q_first, q_second) - value_now
    value_loss = jnp.where(gap < 0.0, 0.3, 0.7) * gap * gap
    return jnp.stack([q_first, q_second]), jnp.stack([value_now, value_next]), targets, q_loss, value_loss
```

```python
import functools

import jax
import jax.numpy as jnp
from jax import lax
from jax.experimental import pallas as pl
from jax.experimental.pallas import tpu as pltpu
from jax.sharding import PartitionSpec as P

MESH = pl.DeviceIdType.MESH
PARTS = 4
LANES = 256
KINDS = 8


def log2(value):
    bits = value.bit_length() - 1
    assert 1 << bits == value
    return bits


def orders_of(dp_size, mp_size):
    mp_bits, dp_bits = log2(mp_size), log2(dp_size)
    last = mp_bits
    first = mp_bits - 1
    others = [b for b in range(mp_bits + dp_bits) if b not in (last, first)]
    orders = []
    for part in range(PARTS):
        turn = part % len(others)
        orders.append([first] + others[turn:] + others[:turn] + [last])
    return orders


def kernel(
    dp_size,
    mp_size,
    buffer,
    owner_ref,
    row_ref,
    q_in_ref,
    q_mid_ref,
    q_out_ref,
    v_in_ref,
    v_mid_ref,
    v_out_ref,
    q_values_ref,
    values_ref,
    targets_ref,
    q_loss_ref,
    value_loss_ref,
    rows_v,
    wide,
    first_w,
    mid_w,
    out_w,
    table,
    hot,
    place,
    load_sem,
    send_sem,
    recv_sem,
    pass_send_sem,
    pass_recv_sem,
):
    f32, bf16 = jnp.float32, jnp.bfloat16
    orders = orders_of(dp_size, mp_size)
    mp_bits = log2(mp_size)
    steps = len(orders[0]) - 1
    half = 1 << steps
    dp, mp = lax.axis_index("dp"), lax.axis_index("mp")
    me = dp * mp_size + mp
    rows_dev = buffer.shape[0]
    part_rows = rows_dev // PARTS
    groups = part_rows // LANES
    states_width = v_in_ref.shape[0]
    pair_width = q_in_ref.shape[1]
    hidden = v_mid_ref.shape[0]
    batch = row_ref.shape[1]

    def load(part):
        span = pl.ds(part * part_rows, part_rows)
        return pltpu.make_async_copy(buffer.at[span], rows_v.at[span], load_sem.at[part])

    for part in range(PARTS):
        load(part).start()

    def partner(bit):
        if bit < mp_bits:
            step = 1 << bit
            return (dp, mp + step * (1 - 2 * ((mp // step) % 2)))
        step = 1 << (bit - mp_bits)
        return (dp + step * (1 - 2 * ((dp // step) % 2)), mp)

    barrier = pltpu.get_barrier_semaphore()
    for bit in sorted(orders[0]):
        pl.semaphore_signal(barrier, inc=1, device_id=partner(bit), device_id_type=MESH)

    def padded(value):
        wide[...] = jnp.zeros_like(wide)
        wide[0 : value.shape[0], :] = value.astype(f32)
        return wide[...].T

    for head in range(2):
        first_w[head * hidden : (head + 1) * hidden, :] = padded(q_in_ref[head]).astype(bf16)
        mid_w[head] = q_mid_ref[head].astype(f32).T.astype(bf16)
    value_w = padded(v_in_ref[...])
    first_w[2 * hidden : 3 * hidden, :] = value_w.astype(bf16)
    first_w[3 * hidden : 4 * hidden, :] = pltpu.roll(value_w, pair_width, 1).astype(bf16)
    mid_w[2] = v_mid_ref[...].astype(f32).T.astype(bf16)
    unit = lax.broadcasted_iota(jnp.int32, (16, LANES), 1)
    pick = lax.broadcasted_iota(jnp.int32, (16, LANES), 0)
    first_w[4 * hidden : 4 * hidden + 16, :] = jnp.where(
        (unit == pick + (pair_width + states_width)) & (pick < 2), 1.0, 0.0
    ).astype(bf16)
    wide[0:2, :] = q_out_ref[...].astype(f32)
    wide[2:3, :] = v_out_ref[...].astype(f32)
    columns = wide[0:8, :].T
    for head in range(3):
        out_w[head] = jnp.broadcast_to(columns[:, head : head + 1], (hidden, 128))

    wanted = row_ref[...]
    relative = owner_ref[...] ^ me
    low = wanted & (LANES - 1)
    group = wanted // LANES
    hot[...] = jnp.where(
        lax.broadcasted_iota(jnp.int32, (LANES, batch), 0) == low, 1.0, 0.0
    ).astype(bf16)
    for part in range(PARTS):
        slot = jnp.zeros_like(relative)
        for position, bit in enumerate(orders[part]):
            slot = slot + (((relative >> bit) & 1) << position)
        here = (group // groups) == part
        index = jnp.where(here, slot * groups + (group - part * groups), -1)
        place[part] = jnp.broadcast_to(index, (KINDS, batch))

    def send(part, step):
        count = 1 << step
        return pltpu.make_async_remote_copy(
            src_ref=table.at[part, pl.ds(0, count)],
            dst_ref=table.at[part, pl.ds(count, count)],
            send_sem=send_sem.at[part, step],
            recv_sem=recv_sem.at[part, step],
            device_id=partner(orders[part][step]),
            device_id_type=MESH,
        )

    def span_of(stage):
        return (0, 1) if stage == 0 else (1 << (stage - 1), 1 << (stage - 1))

    def hand_over(part, stage):
        start, count = span_of(stage)
        return pltpu.make_async_remote_copy(
            src_ref=table.at[part, pl.ds(start, count)],
            dst_ref=table.at[part, pl.ds(half + start, count)],
            send_sem=pass_send_sem.at[part, stage],
            recv_sem=pass_recv_sem.at[part, stage],
            device_id=partner(orders[part][-1]),
            device_id_type=MESH,
        )

    def evaluate(part):
        blocks = []
        for g in range(groups):
            start = part * part_rows + g * LANES
            block = rows_v[start : start + LANES, :]
            ones = lax.dot_general(
                first_w[...], block, (((1,), (1,)), ((), ())), preferred_element_type=f32
            )
            outs = []
            for head in range(4):
                h1 = jnp.maximum(ones[head * hidden : (head + 1) * hidden], 0.0).astype(bf16)
                kind = min(head, 2)
                h2 = jnp.maximum(
                    jnp.dot(mid_w[kind], h1, preferred_element_type=f32), 0.0
                )
                weight = out_w[kind]
                outs.append(
                    jnp.concatenate(
                        [
                            jnp.sum(h2[:, n : n + 128] * weight, axis=0, keepdims=True)
                            for n in range(0, LANES, 128)
                        ],
                        axis=1,
                    )
                )
            reward = ones[4 * hidden : 4 * hidden + 1]
            discount = ones[4 * hidden + 1 : 4 * hidden + 2]
            q_first, q_second, value_now, value_next = outs
            targets = reward + discount * value_next
            q_loss = (q_first - targets) ** 2 + (q_second - targets) ** 2
            gap = jnp.minimum(q_first, q_second) - value_now
            value_loss = jnp.where(gap < 0.0, 0.3, 0.7) * gap * gap
            blocks += [
                q_first,
                q_second,
                value_now,
                value_next,
                targets,
                q_loss,
                value_loss,
                jnp.zeros_like(q_loss),
            ]
        table[part, 0] = jnp.concatenate(blocks, axis=0).astype(bf16)

    def select(acc, part, start, count):
        def some(acc, start, count):
            piece = table[part, pl.ds(start, count)].reshape(count * groups * KINDS, LANES)
            found = jnp.dot(piece, hot[...], preferred_element_type=f32)
            where = place[part]
            for j in range(count * groups):
                acc = jnp.where(
                    where == start * groups + j, found[j * KINDS : (j + 1) * KINDS], acc
                )
            return acc

        if count <= 8:
            return some(acc, start, count)
        return lax.fori_loop(0, count // 8, lambda i, a: some(a, start + i * 8, 8), acc)

    acc = jnp.zeros((KINDS, batch), f32)

    def arrived(part, step):
        send(part, step).wait_recv()
        if step + 1 < steps:
            send(part, step + 1).start()
        hand_over(part, step + 1).start()

    events = sorted(
        ((part * 0.8 + step * 1.8, part, step) for part in range(PARTS) for step in range(steps)),
    )
    pending = list(events)
    for part in range(PARTS):
        load(part).wait()
        evaluate(part)
        if part == 0:
            pl.semaphore_wait(barrier, len(orders[0]))
        send(part, 0).start()
        hand_over(part, 0).start()
        if part >= 2:
            _, p, s = pending.pop(0)
            arrived(p, s)
    for part in range(PARTS):
        acc = select(acc, part, 0, 1)
    for part in range(PARTS):
        hand_over(part, 0).wait_recv()
        acc = select(acc, part, half, 1)
    done = [(p, s) for (_, p, s) in events if not any(q[1:] == (p, s) for q in pending)]
    late = []
    for p, s in done:
        start, count = span_of(s + 1)
        acc = select(acc, p, start, count)
        late.append((p, s))
    for _, p, s in pending:
        arrived(p, s)
        start, count = span_of(s + 1)
        acc = select(acc, p, start, count)
        late.append((p, s))
        if len(late) > 3:
            p, s = late.pop(0)
            hand_over(p, s + 1).wait_recv()
            start, count = span_of(s + 1)
            acc = select(acc, p, half + start, count)
    for p, s in late:
        hand_over(p, s + 1).wait_recv()
        start, count = span_of(s + 1)
        acc = select(acc, p, half + start, count)
    q_values_ref[...] = acc[0:2]
    values_ref[...] = acc[2:4]
    targets_ref[...] = acc[4:5]
    q_loss_ref[...] = acc[5:6]
    value_loss_ref[...] = acc[6:7]
    for part in range(PARTS):
        for step in range(steps):
            send(part, step).wait_send()
        for stage in range(steps + 1):
            hand_over(part, stage).wait_send()


def body(buffer, owner, local_row, q_in, q_mid, q_out, v_in, v_mid, v_out):
    dp_size, mp_size = lax.axis_size("dp"), lax.axis_size("mp")
    owners = dp_size * mp_size
    batch = local_row.shape[0]
    rows_dev, width = buffer.shape
    hidden = v_mid.shape[0]
    assert width == LANES and hidden == LANES
    groups = rows_dev // PARTS // LANES
    steps = log2(owners) - 1
    f32, bf16 = jnp.float32, jnp.bfloat16
    vmem = pl.BlockSpec(memory_space=pltpu.VMEM)
    outs = pl.pallas_call(
        functools.partial(kernel, dp_size, mp_size),
        out_shape=(
            jax.ShapeDtypeStruct((2, batch), f32),
            jax.ShapeDtypeStruct((2, batch), f32),
            jax.ShapeDtypeStruct((1, batch), f32),
            jax.ShapeDtypeStruct((1, batch), f32),
            jax.ShapeDtypeStruct((1, batch), f32),
        ),
        in_specs=[pl.BlockSpec(memory_space=pl.ANY)] + [vmem] * 8,
        out_specs=(vmem,) * 5,
        scratch_shapes=[
            pltpu.VMEM((rows_dev, width), bf16),
            pltpu.VMEM((width, hidden), f32),
            pltpu.VMEM((4 * hidden + 16, width), bf16),
            pltpu.VMEM((3, hidden, hidden), bf16),
            pltpu.VMEM((3, hidden, 128), f32),
            pltpu.VMEM((PARTS, owners, groups * KINDS, LANES), bf16),
            pltpu.VMEM((LANES, batch), bf16),
            pltpu.VMEM((PARTS, KINDS, batch), jnp.int32),
            pltpu.SemaphoreType.DMA((PARTS,)),
            pltpu.SemaphoreType.DMA((PARTS, steps)),
            pltpu.SemaphoreType.DMA((PARTS, steps)),
            pltpu.SemaphoreType.DMA((PARTS, steps + 1)),
            pltpu.SemaphoreType.DMA((PARTS, steps + 1)),
        ],
        compiler_params=pltpu.CompilerParams(
            collective_id=0, has_side_effects=True, vmem_limit_bytes=48 << 20
        ),
        name="critic_exchange",
    )(
        buffer,
        owner.reshape(1, batch),
        local_row.reshape(1, batch),
        q_in,
        q_mid,
        q_out,
        v_in,
        v_mid,
        v_out.reshape(1, hidden),
    )
    q_values, values, targets, q_loss, value_loss = outs
    return (
        q_values,
        values,
        targets.reshape(batch),
        q_loss.reshape(batch),
        value_loss.reshape(batch),
    )


def solution(mesh):
    return jax.shard_map(
        body,
        mesh=mesh,
        in_specs=(
            P(("dp", "mp"), None),
            P(("dp", "mp"), None),
            P(("dp", "mp")),
            P(),
            P(),
            P(),
            P(),
            P(),
            P(),
        ),
        out_specs=(
            P(None, ("dp", "mp")),
            P(None, ("dp", "mp")),
            P(("dp", "mp")),
            P(("dp", "mp")),
            P(("dp", "mp")),
        ),
        check_vma=False,
    )
```

```python
import functools

import jax
import jax.numpy as jnp
from jax import lax
from jax.experimental import pallas as pl
from jax.experimental.pallas import tpu as pltpu
from jax.sharding import PartitionSpec as P

MESH = pl.DeviceIdType.MESH
PARTS = 4
LANES = 256
KINDS = 8


def log2(value):
    bits = value.bit_length() - 1
    assert 1 << bits == value
    return bits


def orders_of(dp_size, mp_size):
    mp_bits, dp_bits = log2(mp_size), log2(dp_size)
    last = mp_bits
    first = mp_bits - 1
    others = [b for b in range(mp_bits + dp_bits) if b not in (last, first)]
    orders = []
    for part in range(PARTS):
        turn = part % len(others)
        orders.append([first] + others[turn:] + others[:turn] + [last])
    return orders


def kernel(
    dp_size,
    mp_size,
    buffer,
    owner_hbm,
    row_hbm,
    q_in_hbm,
    q_mid_hbm,
    q_out_hbm,
    v_in_hbm,
    v_mid_hbm,
    v_out_hbm,
    result_ref,
    owner_ref,
    row_ref,
    q_in_ref,
    q_mid_ref,
    q_out_ref,
    v_in_ref,
    v_mid_ref,
    v_out_ref,
    rows_v,
    wide,
    first_w,
    mid_w,
    out_w,
    table,
    hot,
    place,
    load_sem,
    fetch_sem,
    send_sem,
    recv_sem,
    pass_send_sem,
    pass_recv_sem,
):
    f32, bf16 = jnp.float32, jnp.bfloat16
    orders = orders_of(dp_size, mp_size)
    mp_bits = log2(mp_size)
    steps = len(orders[0]) - 1
    half = 1 << steps
    dp, mp = lax.axis_index("dp"), lax.axis_index("mp")
    me = dp * mp_size + mp
    rows_dev = buffer.shape[0]
    part_rows = rows_dev // PARTS
    groups = part_rows // LANES
    states_width = v_in_ref.shape[0]
    pair_width = q_in_ref.shape[0]
    hidden = v_mid_ref.shape[0]
    batch = row_ref.shape[1]

    def load(part):
        span = pl.ds(part * part_rows, part_rows)
        return pltpu.make_async_copy(buffer.at[span], rows_v.at[span], load_sem.at[part])

    fetches = [
        pltpu.make_async_copy(source, target, fetch_sem.at[number])
        for number, (source, target) in enumerate(
            (
                (q_in_hbm, q_in_ref),
                (v_in_hbm, v_in_ref),
                (q_mid_hbm, q_mid_ref),
                (v_mid_hbm, v_mid_ref),
                (q_out_hbm, q_out_ref),
                (v_out_hbm, v_out_ref),
                (owner_hbm, owner_ref),
                (row_hbm, row_ref),
            )
        )
    ]
    for fetch in fetches:
        fetch.start()
    for part in range(PARTS):
        load(part).start()

    def partner(bit):
        if bit < mp_bits:
            step = 1 << bit
            return (dp, mp + step * (1 - 2 * ((mp // step) % 2)))
        step = 1 << (bit - mp_bits)
        return (dp + step * (1 - 2 * ((dp // step) % 2)), mp)

    barrier = pltpu.get_barrier_semaphore()
    for bit in sorted(orders[0]):
        pl.semaphore_signal(barrier, inc=1, device_id=partner(bit), device_id_type=MESH)

    def padded(value):
        wide[...] = jnp.zeros_like(wide)
        wide[0 : value.shape[0], :] = value.astype(f32)
        return wide[...].T

    for fetch in fetches:
        fetch.wait()
    for head in range(2):
        first_w[head * hidden : (head + 1) * hidden, :] = padded(q_in_ref[:, head, :]).astype(bf16)
        mid_w[head] = q_mid_ref[head].astype(f32).T.astype(bf16)
    value_w = padded(v_in_ref[...])
    first_w[2 * hidden : 3 * hidden, :] = value_w.astype(bf16)
    first_w[3 * hidden : 4 * hidden, :] = pltpu.roll(value_w, pair_width, 1).astype(bf16)
    mid_w[2] = v_mid_ref[...].astype(f32).T.astype(bf16)
    unit = lax.broadcasted_iota(jnp.int32, (16, LANES), 1)
    pick = lax.broadcasted_iota(jnp.int32, (16, LANES), 0)
    first_w[4 * hidden : 4 * hidden + 16, :] = jnp.where(
        (unit == pick + (pair_width + states_width)) & (pick < 2), 1.0, 0.0
    ).astype(bf16)
    wide[0:2, :] = q_out_ref[...].astype(f32)
    wide[2:3, :] = v_out_ref[...].astype(f32).reshape(1, hidden)
    columns = wide[0:8, :].T
    for head in range(3):
        out_w[head] = jnp.broadcast_to(columns[:, head : head + 1], (hidden, 128))

    wanted = row_ref[...]
    relative = owner_ref[...] ^ me
    low = wanted & (LANES - 1)
    group = wanted // LANES
    hot[...] = jnp.where(
        lax.broadcasted_iota(jnp.int32, (LANES, batch), 0) == low, 1.0, 0.0
    ).astype(bf16)
    for part in range(PARTS):
        slot = jnp.zeros_like(relative)
        for position, bit in enumerate(orders[part]):
            slot = slot + (((relative >> bit) & 1) << position)
        here = (group // groups) == part
        index = jnp.where(here, slot * groups + (group - part * groups), -1)
        place[part] = jnp.broadcast_to(index, (KINDS, batch))

    def send(part, step):
        count = 1 << step
        return pltpu.make_async_remote_copy(
            src_ref=table.at[part, pl.ds(0, count)],
            dst_ref=table.at[part, pl.ds(count, count)],
            send_sem=send_sem.at[part, step],
            recv_sem=recv_sem.at[part, step],
            device_id=partner(orders[part][step]),
            device_id_type=MESH,
        )

    def span_of(stage):
        return (0, 1) if stage == 0 else (1 << (stage - 1), 1 << (stage - 1))

    def hand_over(part, stage):
        start, count = span_of(stage)
        return pltpu.make_async_remote_copy(
            src_ref=table.at[part, pl.ds(start, count)],
            dst_ref=table.at[part, pl.ds(half + start, count)],
            send_sem=pass_send_sem.at[part, stage],
            recv_sem=pass_recv_sem.at[part, stage],
            device_id=partner(orders[part][-1]),
            device_id_type=MESH,
        )

    def evaluate(part):
        blocks = []
        for g in range(groups):
            start = part * part_rows + g * LANES
            block = rows_v[start : start + LANES, :]
            ones = lax.dot_general(
                first_w[...], block, (((1,), (1,)), ((), ())), preferred_element_type=f32
            )
            outs = []
            for head in range(4):
                h1 = jnp.maximum(ones[head * hidden : (head + 1) * hidden], 0.0).astype(bf16)
                kind = min(head, 2)
                h2 = jnp.maximum(
                    jnp.dot(mid_w[kind], h1, preferred_element_type=f32), 0.0
                )
                weight = out_w[kind]
                outs.append(
                    jnp.concatenate(
                        [
                            jnp.sum(h2[:, n : n + 128] * weight, axis=0, keepdims=True)
                            for n in range(0, LANES, 128)
                        ],
                        axis=1,
                    )
                )
            reward = ones[4 * hidden : 4 * hidden + 1]
            discount = ones[4 * hidden + 1 : 4 * hidden + 2]
            q_first, q_second, value_now, value_next = outs
            targets = reward + discount * value_next
            q_loss = (q_first - targets) ** 2 + (q_second - targets) ** 2
            gap = jnp.minimum(q_first, q_second) - value_now
            value_loss = jnp.where(gap < 0.0, 0.3, 0.7) * gap * gap
            blocks += [
                q_first,
                q_second,
                value_now,
                value_next,
                targets,
                q_loss,
                value_loss,
                jnp.zeros_like(q_loss),
            ]
        table[part, 0] = jnp.concatenate(blocks, axis=0).astype(bf16)

    def select(acc, part, start, count):
        def some(acc, start, count):
            piece = table[part, pl.ds(start, count)].reshape(count * groups * KINDS, LANES)
            found = jnp.dot(piece, hot[...], preferred_element_type=f32)
            where = place[part]
            for j in range(count * groups):
                acc = jnp.where(
                    where == start * groups + j, found[j * KINDS : (j + 1) * KINDS], acc
                )
            return acc

        if count <= 8:
            return some(acc, start, count)
        return lax.fori_loop(0, count // 8, lambda i, a: some(a, start + i * 8, 8), acc)

    acc = jnp.zeros((KINDS, batch), f32)

    def arrived(part, step):
        send(part, step).wait_recv()
        if step + 1 < steps:
            send(part, step + 1).start()
        hand_over(part, step + 1).start()

    events = sorted(
        ((part * 0.8 + step * 1.8, part, step) for part in range(PARTS) for step in range(steps)),
    )
    pending = list(events)
    for part in range(PARTS):
        load(part).wait()
        evaluate(part)
        if part == 0:
            pl.semaphore_wait(barrier, len(orders[0]))
        send(part, 0).start()
        hand_over(part, 0).start()
        if part >= 2:
            _, p, s = pending.pop(0)
            arrived(p, s)
    for part in range(PARTS):
        acc = select(acc, part, 0, 1)
    for part in range(PARTS):
        hand_over(part, 0).wait_recv()
        acc = select(acc, part, half, 1)
    done = [(p, s) for (_, p, s) in events if not any(q[1:] == (p, s) for q in pending)]
    late = []
    for p, s in done:
        start, count = span_of(s + 1)
        acc = select(acc, p, start, count)
        late.append((p, s))
    for _, p, s in pending:
        arrived(p, s)
        start, count = span_of(s + 1)
        acc = select(acc, p, start, count)
        late.append((p, s))
        if len(late) > 3:
            p, s = late.pop(0)
            hand_over(p, s + 1).wait_recv()
            start, count = span_of(s + 1)
            acc = select(acc, p, half + start, count)
    for p, s in late:
        hand_over(p, s + 1).wait_recv()
        start, count = span_of(s + 1)
        acc = select(acc, p, half + start, count)
    result_ref[...] = acc
    for part in range(PARTS):
        for step in range(steps):
            send(part, step).wait_send()
        for stage in range(steps + 1):
            hand_over(part, stage).wait_send()


def spread(result_ref, q_values_ref, values_ref, targets_ref, q_loss_ref, value_loss_ref):
    q_values_ref[...] = result_ref[0:2]
    values_ref[...] = result_ref[2:4]
    targets_ref[...] = result_ref[4:5]
    q_loss_ref[...] = result_ref[5:6]
    value_loss_ref[...] = result_ref[6:7]


def body(buffer, owner, local_row, q_in, q_mid, q_out, v_in, v_mid, v_out):
    dp_size, mp_size = lax.axis_size("dp"), lax.axis_size("mp")
    owners = dp_size * mp_size
    batch = local_row.shape[0]
    rows_dev, width = buffer.shape
    hidden = v_mid.shape[0]
    assert width == LANES and hidden == LANES
    groups = rows_dev // PARTS // LANES
    steps = log2(owners) - 1
    f32, bf16 = jnp.float32, jnp.bfloat16
    vmem = pl.BlockSpec(memory_space=pltpu.VMEM)
    hbm = pl.BlockSpec(memory_space=pltpu.HBM)
    result = pl.pallas_call(
        functools.partial(kernel, dp_size, mp_size),
        out_shape=pltpu.VMEM((KINDS, batch), f32),
        in_specs=[hbm] * 9,
        out_specs=vmem,
        scratch_shapes=[
            pltpu.VMEM((1, batch), jnp.int32),
            pltpu.VMEM((1, batch), jnp.int32),
            pltpu.VMEM((q_in.shape[1], 2, hidden), bf16),
            pltpu.VMEM(q_mid.shape, bf16),
            pltpu.VMEM(q_out.shape, bf16),
            pltpu.VMEM(v_in.shape, bf16),
            pltpu.VMEM(v_mid.shape, bf16),
            pltpu.VMEM(v_out.shape, bf16),
            pltpu.VMEM((rows_dev, width), bf16),
            pltpu.VMEM((width, hidden), f32),
            pltpu.VMEM((4 * hidden + 16, width), bf16),
            pltpu.VMEM((3, hidden, hidden), bf16),
            pltpu.VMEM((3, hidden, 128), f32),
            pltpu.VMEM((PARTS, owners, groups * KINDS, LANES), bf16),
            pltpu.VMEM((LANES, batch), bf16),
            pltpu.VMEM((PARTS, KINDS, batch), jnp.int32),
            pltpu.SemaphoreType.DMA((PARTS,)),
            pltpu.SemaphoreType.DMA((8,)),
            pltpu.SemaphoreType.DMA((PARTS, steps)),
            pltpu.SemaphoreType.DMA((PARTS, steps)),
            pltpu.SemaphoreType.DMA((PARTS, steps + 1)),
            pltpu.SemaphoreType.DMA((PARTS, steps + 1)),
        ],
        compiler_params=pltpu.CompilerParams(
            collective_id=0, has_side_effects=True, vmem_limit_bytes=48 << 20
        ),
        name="critic_exchange",
    )(
        *(
            pltpu.with_memory_space_constraint(x, pltpu.HBM)
            for x in (
                buffer,
                owner.reshape(1, batch),
                local_row.reshape(1, batch),
                jnp.transpose(q_in, (1, 0, 2)),
                q_mid,
                q_out,
                v_in,
                v_mid,
                v_out,
            )
        )
    )
    one = jax.ShapeDtypeStruct((1, batch), f32)
    two = jax.ShapeDtypeStruct((2, batch), f32)
    outs = pl.pallas_call(
        spread,
        out_shape=(two, two, one, one, one),
        in_specs=[vmem],
        out_specs=(vmem,) * 5,
        compiler_params=pltpu.CompilerParams(vmem_limit_bytes=1 << 20),
        name="spread",
    )(result)
    q_values, values, targets, q_loss, value_loss = outs
    return (
        q_values,
        values,
        targets.reshape(batch),
        q_loss.reshape(batch),
        value_loss.reshape(batch),
    )


def solution(mesh):
    return jax.shard_map(
        body,
        mesh=mesh,
        in_specs=(
            P(("dp", "mp"), None),
            P(("dp", "mp"), None),
            P(("dp", "mp")),
            P(),
            P(),
            P(),
            P(),
            P(),
            P(),
        ),
        out_specs=(
            P(None, ("dp", "mp")),
            P(None, ("dp", "mp")),
            P(("dp", "mp")),
            P(("dp", "mp")),
            P(("dp", "mp")),
        ),
        check_vma=False,
    )
```

```python
import functools

import jax
import jax.numpy as jnp
from jax import lax
from jax.experimental import pallas as pl
from jax.experimental.pallas import tpu as pltpu
from jax.sharding import PartitionSpec as P

MESH = pl.DeviceIdType.MESH
PARTS = 2
LANES = 256
KINDS = 8
EVERY, STAGE, HOP, BEHIND = 0.9, 2.4, 0.8, 6


def log2(value):
    bits = value.bit_length() - 1
    assert 1 << bits == value
    return bits


def plan_of(dp_size, mp_size):
    mp_bits, dp_bits = log2(mp_size), log2(dp_size)
    last = mp_bits
    inner = list(range(mp_bits))
    outer = [b for b in range(mp_bits, mp_bits + dp_bits) if b != last]
    stages = [bits[n : n + 2] for bits in (inner, outer) for n in range(0, len(bits), 2)]
    return [(stages, last) for _ in range(PARTS)]


def pieces_of(stages):
    pieces, count = [], 1
    for number, bits in enumerate(stages):
        combos = range(1, 1 << len(bits))
        for combo in sorted(combos, key=lambda c: (c.bit_count(), c)):
            mask = sum(1 << b for n, b in enumerate(bits) if (combo >> n) & 1)
            pieces.append((number, mask, combo * count, count))
        count <<= len(bits)
    return pieces, count


def kernel(
    dp_size,
    mp_size,
    buffer,
    owner_hbm,
    row_hbm,
    q_in_hbm,
    q_mid_hbm,
    q_out_hbm,
    v_in_hbm,
    v_mid_hbm,
    v_out_hbm,
    result_ref,
    owner_ref,
    row_ref,
    q_in_ref,
    q_mid_ref,
    q_out_ref,
    v_in_ref,
    v_mid_ref,
    v_out_ref,
    rows_v,
    wide,
    first_w,
    mid_w,
    out_w,
    table,
    hot,
    place,
    load_sem,
    fetch_sem,
    send_sem,
    recv_sem,
    pass_send_sem,
    pass_recv_sem,
):
    f32, bf16 = jnp.float32, jnp.bfloat16
    plan = plan_of(dp_size, mp_size)
    mp_bits = log2(mp_size)
    pieces = [pieces_of(stages)[0] for stages, _ in plan]
    half = pieces_of(plan[0][0])[1]
    dp, mp = lax.axis_index("dp"), lax.axis_index("mp")
    me = dp * mp_size + mp
    rows_dev = buffer.shape[0]
    part_rows = rows_dev // PARTS
    groups = part_rows // LANES
    states_width = v_in_ref.shape[0]
    pair_width = q_in_ref.shape[0]
    hidden = v_mid_ref.shape[0]
    batch = row_ref.shape[1]

    def load(part):
        span = pl.ds(part * part_rows, part_rows)
        return pltpu.make_async_copy(buffer.at[span], rows_v.at[span], load_sem.at[part])

    fetches = [
        pltpu.make_async_copy(source, target, fetch_sem.at[number])
        for number, (source, target) in enumerate(
            (
                (q_in_hbm, q_in_ref),
                (v_in_hbm, v_in_ref),
                (q_mid_hbm, q_mid_ref),
                (v_mid_hbm, v_mid_ref),
                (q_out_hbm, q_out_ref),
                (v_out_hbm, v_out_ref),
                (owner_hbm, owner_ref),
                (row_hbm, row_ref),
            )
        )
    ]
    for fetch in fetches:
        fetch.start()
    for part in range(PARTS):
        load(part).start()

    def partner(mask):
        there = [mp, dp]
        for bit in range(mask.bit_length()):
            if (mask >> bit) & 1:
                axis, step = (0, 1 << bit) if bit < mp_bits else (1, 1 << (bit - mp_bits))
                there[axis] = there[axis] + step * (1 - 2 * ((there[axis] // step) % 2))
        return (there[1], there[0])

    partners = {mask for sends in pieces for _, mask, _, _ in sends}
    partners |= {1 << last for _, last in plan if last is not None}
    barrier = pltpu.get_barrier_semaphore()
    for mask in sorted(partners):
        pl.semaphore_signal(barrier, inc=1, device_id=partner(mask), device_id_type=MESH)

    def padded(value):
        wide[...] = jnp.zeros_like(wide)
        wide[0 : value.shape[0], :] = value.astype(f32)
        return wide[...].T

    for fetch in fetches:
        fetch.wait()
    for head in range(2):
        first_w[head * hidden : (head + 1) * hidden, :] = padded(q_in_ref[:, head, :]).astype(bf16)
        mid_w[head] = q_mid_ref[head].astype(f32).T.astype(bf16)
    value_w = padded(v_in_ref[...])
    first_w[2 * hidden : 3 * hidden, :] = value_w.astype(bf16)
    first_w[3 * hidden : 4 * hidden, :] = pltpu.roll(value_w, pair_width, 1).astype(bf16)
    mid_w[2] = v_mid_ref[...].astype(f32).T.astype(bf16)
    unit = lax.broadcasted_iota(jnp.int32, (16, LANES), 1)
    pick = lax.broadcasted_iota(jnp.int32, (16, LANES), 0)
    first_w[4 * hidden : 4 * hidden + 16, :] = jnp.where(
        (unit == pick + (pair_width + states_width)) & (pick < 2), 1.0, 0.0
    ).astype(bf16)
    wide[0:2, :] = q_out_ref[...].astype(f32)
    wide[2:3, :] = v_out_ref[...].astype(f32).reshape(1, hidden)
    columns = wide[0:8, :].T
    for head in range(3):
        out_w[head] = jnp.broadcast_to(columns[:, head : head + 1], (hidden, 128))

    wanted = row_ref[...]
    relative = owner_ref[...] ^ me
    low = wanted & (LANES - 1)
    group = wanted // LANES
    hot[...] = jnp.where(
        lax.broadcasted_iota(jnp.int32, (LANES, batch), 0) == low, 1.0, 0.0
    ).astype(bf16)
    for part in range(PARTS):
        slot = jnp.zeros_like(relative)
        stages, last = plan[part]
        bits = [bit for stage in stages for bit in stage]
        for position, bit in enumerate(bits + ([] if last is None else [last])):
            slot = slot + (((relative >> bit) & 1) << position)
        here = (group // groups) == part
        index = jnp.where(here, slot * groups + (group - part * groups), -1)
        place[part] = jnp.broadcast_to(index, (KINDS, batch))

    def send(part, number):
        _, mask, start, count = pieces[part][number]
        return pltpu.make_async_remote_copy(
            src_ref=table.at[part, pl.ds(0, count)],
            dst_ref=table.at[part, pl.ds(start, count)],
            send_sem=send_sem.at[part, number],
            recv_sem=recv_sem.at[part, number],
            device_id=partner(mask),
            device_id_type=MESH,
        )

    def hand_over(part, number):
        start, count = (0, 1) if number < 0 else pieces[part][number][2:]
        return pltpu.make_async_remote_copy(
            src_ref=table.at[part, pl.ds(start, count)],
            dst_ref=table.at[part, pl.ds(half + start, count)],
            send_sem=pass_send_sem.at[part, number + 1],
            recv_sem=pass_recv_sem.at[part, number + 1],
            device_id=partner(1 << plan[part][1]),
            device_id_type=MESH,
        )

    def evaluate(part):
        blocks = []
        for g in range(groups):
            start = part * part_rows + g * LANES
            block = rows_v[start : start + LANES, :]
            ones = lax.dot_general(
                first_w[...], block, (((1,), (1,)), ((), ())), preferred_element_type=f32
            )
            outs = []
            for head in range(4):
                h1 = jnp.maximum(ones[head * hidden : (head + 1) * hidden], 0.0).astype(bf16)
                kind = min(head, 2)
                h2 = jnp.maximum(
                    jnp.dot(mid_w[kind], h1, preferred_element_type=f32), 0.0
                )
                weight = out_w[kind]
                outs.append(
                    jnp.concatenate(
                        [
                            jnp.sum(h2[:, n : n + 128] * weight, axis=0, keepdims=True)
                            for n in range(0, LANES, 128)
                        ],
                        axis=1,
                    )
                )
            reward = ones[4 * hidden : 4 * hidden + 1]
            discount = ones[4 * hidden + 1 : 4 * hidden + 2]
            q_first, q_second, value_now, value_next = outs
            targets = reward + discount * value_next
            q_loss = (q_first - targets) ** 2 + (q_second - targets) ** 2
            gap = jnp.minimum(q_first, q_second) - value_now
            value_loss = jnp.where(gap < 0.0, 0.3, 0.7) * gap * gap
            blocks += [
                q_first,
                q_second,
                value_now,
                value_next,
                targets,
                q_loss,
                value_loss,
                jnp.zeros_like(q_loss),
            ]
        table[part, 0] = jnp.concatenate(blocks, axis=0).astype(bf16)

    def select(acc, part, start, count):
        def some(acc, start, count):
            piece = table[part, pl.ds(start, count)].reshape(count * groups * KINDS, LANES)
            found = jnp.dot(piece, hot[...], preferred_element_type=f32)
            where = place[part]
            for j in range(count * groups):
                acc = jnp.where(
                    where == start * groups + j, found[j * KINDS : (j + 1) * KINDS], acc
                )
            return acc

        if count <= 8:
            return some(acc, start, count)
        return lax.fori_loop(0, count // 8, lambda i, a: some(a, start + i * 8, 8), acc)

    acc = jnp.zeros((KINDS, batch), f32)

    def begin(part, stage):
        for number, piece in enumerate(pieces[part]):
            if piece[0] == stage:
                send(part, number).start()

    events = []
    for part in range(PARTS):
        for number, (stage, mask, _, _) in enumerate(pieces[part]):
            when = part * EVERY + stage * STAGE + mask.bit_count() * HOP
            events.append((when, part, number))
    events.sort()
    ready = {}

    def receive(part, number):
        send(part, number).wait_recv()
        stage = pieces[part][number][0]
        ready[part, stage] = ready.get((part, stage), 0) + 1
        if ready[part, stage] == sum(piece[0] == stage for piece in pieces[part]):
            begin(part, stage + 1)
        if plan[part][1] is not None:
            hand_over(part, number).start()

    taken = []
    late = []
    for part in range(PARTS):
        load(part).wait()
        evaluate(part)
        if part == 0:
            pl.semaphore_wait(barrier, len(partners))
        begin(part, 0)
        if plan[part][1] is not None:
            hand_over(part, -1).start()
            late.append((part, -1))
        while events and events[0][0] < (part - 1) * EVERY:
            _, p, n = events.pop(0)
            receive(p, n)
            taken.append((p, n))
    for part in range(PARTS):
        acc = select(acc, part, 0, 1)
    for p, n in taken:
        acc = select(acc, p, *pieces[p][n][2:])
        if plan[p][1] is not None:
            late.append((p, n))

    def finish(acc, part, number):
        hand_over(part, number).wait_recv()
        start, count = (0, 1) if number < 0 else pieces[part][number][2:]
        return select(acc, part, half + start, count)

    for _, p, n in events:
        receive(p, n)
        acc = select(acc, p, *pieces[p][n][2:])
        if plan[p][1] is not None:
            late.append((p, n))
        if len(late) > BEHIND:
            acc = finish(acc, *late.pop(0))
    for p, n in late:
        acc = finish(acc, p, n)
    result_ref[...] = acc
    for part in range(PARTS):
        for number in range(len(pieces[part])):
            send(part, number).wait_send()
        if plan[part][1] is not None:
            for number in range(-1, len(pieces[part])):
                hand_over(part, number).wait_send()


def spread(result_ref, q_values_ref, values_ref, targets_ref, q_loss_ref, value_loss_ref):
    q_values_ref[...] = result_ref[0:2]
    values_ref[...] = result_ref[2:4]
    targets_ref[...] = result_ref[4:5]
    q_loss_ref[...] = result_ref[5:6]
    value_loss_ref[...] = result_ref[6:7]


def body(buffer, owner, local_row, q_in, q_mid, q_out, v_in, v_mid, v_out):
    dp_size, mp_size = lax.axis_size("dp"), lax.axis_size("mp")
    owners = dp_size * mp_size
    batch = local_row.shape[0]
    rows_dev, width = buffer.shape
    hidden = v_mid.shape[0]
    assert width == LANES and hidden == LANES
    groups = rows_dev // PARTS // LANES
    sends = max(len(pieces_of(stages)[0]) for stages, _ in plan_of(dp_size, mp_size))
    f32, bf16 = jnp.float32, jnp.bfloat16
    vmem = pl.BlockSpec(memory_space=pltpu.VMEM)
    hbm = pl.BlockSpec(memory_space=pltpu.HBM)
    result = pl.pallas_call(
        functools.partial(kernel, dp_size, mp_size),
        out_shape=pltpu.VMEM((KINDS, batch), f32),
        in_specs=[hbm] * 9,
        out_specs=vmem,
        scratch_shapes=[
            pltpu.VMEM((1, batch), jnp.int32),
            pltpu.VMEM((1, batch), jnp.int32),
            pltpu.VMEM((q_in.shape[1], 2, hidden), bf16),
            pltpu.VMEM(q_mid.shape, bf16),
            pltpu.VMEM(q_out.shape, bf16),
            pltpu.VMEM(v_in.shape, bf16),
            pltpu.VMEM(v_mid.shape, bf16),
            pltpu.VMEM(v_out.shape, bf16),
            pltpu.VMEM((rows_dev, width), bf16),
            pltpu.VMEM((width, hidden), f32),
            pltpu.VMEM((4 * hidden + 16, width), bf16),
            pltpu.VMEM((3, hidden, hidden), bf16),
            pltpu.VMEM((3, hidden, 128), f32),
            pltpu.VMEM((PARTS, owners, groups * KINDS, LANES), bf16),
            pltpu.VMEM((LANES, batch), bf16),
            pltpu.VMEM((PARTS, KINDS, batch), jnp.int32),
            pltpu.SemaphoreType.DMA((PARTS,)),
            pltpu.SemaphoreType.DMA((8,)),
            pltpu.SemaphoreType.DMA((PARTS, sends)),
            pltpu.SemaphoreType.DMA((PARTS, sends)),
            pltpu.SemaphoreType.DMA((PARTS, sends + 1)),
            pltpu.SemaphoreType.DMA((PARTS, sends + 1)),
        ],
        compiler_params=pltpu.CompilerParams(
            collective_id=0, has_side_effects=True, vmem_limit_bytes=48 << 20
        ),
        name="critic_exchange",
    )(
        *(
            pltpu.with_memory_space_constraint(x, pltpu.HBM)
            for x in (
                buffer,
                owner.reshape(1, batch),
                local_row.reshape(1, batch),
                jnp.transpose(q_in, (1, 0, 2)),
                q_mid,
                q_out,
                v_in,
                v_mid,
                v_out,
            )
        )
    )
    one = jax.ShapeDtypeStruct((1, batch), f32)
    two = jax.ShapeDtypeStruct((2, batch), f32)
    outs = pl.pallas_call(
        spread,
        out_shape=(two, two, one, one, one),
        in_specs=[vmem],
        out_specs=(vmem,) * 5,
        compiler_params=pltpu.CompilerParams(vmem_limit_bytes=1 << 20),
        name="spread",
    )(result)
    q_values, values, targets, q_loss, value_loss = outs
    return (
        q_values,
        values,
        targets.reshape(batch),
        q_loss.reshape(batch),
        value_loss.reshape(batch),
    )


def solution(mesh):
    return jax.shard_map(
        body,
        mesh=mesh,
        in_specs=(
            P(("dp", "mp"), None),
            P(("dp", "mp"), None),
            P(("dp", "mp")),
            P(),
            P(),
            P(),
            P(),
            P(),
            P(),
        ),
        out_specs=(
            P(None, ("dp", "mp")),
            P(None, ("dp", "mp")),
            P(("dp", "mp")),
            P(("dp", "mp")),
            P(("dp", "mp")),
        ),
        check_vma=False,
    )
```

```python
import functools
import itertools

import jax
import jax.numpy as jnp
from jax import lax
from jax.experimental import pallas as pl
from jax.experimental.pallas import tpu as pltpu
from jax.sharding import PartitionSpec as P

MESH = pl.DeviceIdType.MESH
PARTS = 2
LANES = 256
KINDS = 8
EVERY, STAGE, HOP, BEHIND = 0.9, 2.4, 0.8, 2


def log2(value):
    bits = value.bit_length() - 1
    assert 1 << bits == value
    return bits


def plan_of(dp_size, mp_size):
    mp_bits, dp_bits = log2(mp_size), log2(dp_size)
    last = mp_bits
    inner = list(range(mp_bits))
    outer = [b for b in range(mp_bits, mp_bits + dp_bits) if b != last]
    plan = []
    for part in range(PARTS):
        turn = part % max(1, len(outer))
        pairs = itertools.zip_longest(inner[::-1], outer[turn:] + outer[:turn])
        plan.append(([[b for b in pair if b is not None] for pair in pairs], last))
    return plan


def pieces_of(stages):
    pieces, count = [], 1
    for number, bits in enumerate(stages):
        combos = range(1, 1 << len(bits))
        for combo in sorted(combos, key=lambda c: (c.bit_count(), c)):
            mask = sum(1 << b for n, b in enumerate(bits) if (combo >> n) & 1)
            pieces.append((number, mask, combo * count, count))
        count <<= len(bits)
    return pieces, count


def kernel(
    dp_size,
    mp_size,
    buffer,
    owner_hbm,
    row_hbm,
    q_in_hbm,
    q_mid_hbm,
    q_out_hbm,
    v_in_hbm,
    v_mid_hbm,
    v_out_hbm,
    result_ref,
    owner_ref,
    row_ref,
    q_in_ref,
    q_mid_ref,
    q_out_ref,
    v_in_ref,
    v_mid_ref,
    v_out_ref,
    rows_v,
    wide,
    first_w,
    mid_w,
    out_w,
    table,
    hot,
    place,
    load_sem,
    fetch_sem,
    send_sem,
    recv_sem,
    pass_send_sem,
    pass_recv_sem,
):
    f32, bf16 = jnp.float32, jnp.bfloat16
    plan = plan_of(dp_size, mp_size)
    mp_bits = log2(mp_size)
    pieces = [pieces_of(stages)[0] for stages, _ in plan]
    half = pieces_of(plan[0][0])[1]
    dp, mp = lax.axis_index("dp"), lax.axis_index("mp")
    me = dp * mp_size + mp
    rows_dev = buffer.shape[0]
    part_rows = rows_dev // PARTS
    groups = part_rows // LANES
    states_width = v_in_ref.shape[0]
    pair_width = q_in_ref.shape[0]
    hidden = v_mid_ref.shape[0]
    batch = row_ref.shape[1]

    def load(part):
        span = pl.ds(part * part_rows, part_rows)
        return pltpu.make_async_copy(buffer.at[span], rows_v.at[span], load_sem.at[part])

    fetches = [
        pltpu.make_async_copy(source, target, fetch_sem.at[number])
        for number, (source, target) in enumerate(
            (
                (q_in_hbm, q_in_ref),
                (v_in_hbm, v_in_ref),
                (q_mid_hbm, q_mid_ref),
                (v_mid_hbm, v_mid_ref),
                (q_out_hbm, q_out_ref),
                (v_out_hbm, v_out_ref),
                (owner_hbm, owner_ref),
                (row_hbm, row_ref),
            )
        )
    ]
    for fetch in fetches:
        fetch.start()
    for part in range(PARTS):
        load(part).start()

    def partner(mask):
        there = [mp, dp]
        for bit in range(mask.bit_length()):
            if (mask >> bit) & 1:
                axis, step = (0, 1 << bit) if bit < mp_bits else (1, 1 << (bit - mp_bits))
                there[axis] = there[axis] + step * (1 - 2 * ((there[axis] // step) % 2))
        return (there[1], there[0])

    partners = {mask for sends in pieces for _, mask, _, _ in sends}
    partners |= {1 << last for _, last in plan if last is not None}
    barrier = pltpu.get_barrier_semaphore()
    for mask in sorted(partners):
        pl.semaphore_signal(barrier, inc=1, device_id=partner(mask), device_id_type=MESH)

    def padded(value):
        wide[...] = jnp.zeros_like(wide)
        wide[0 : value.shape[0], :] = value.astype(f32)
        return wide[...].T

    for fetch in fetches[:6]:
        fetch.wait()
    for head in range(2):
        first_w[head * hidden : (head + 1) * hidden, :] = padded(q_in_ref[:, head, :]).astype(bf16)
        mid_w[head] = q_mid_ref[head].astype(f32).T.astype(bf16)
    value_w = padded(v_in_ref[...])
    first_w[2 * hidden : 3 * hidden, :] = value_w.astype(bf16)
    first_w[3 * hidden : 4 * hidden, :] = pltpu.roll(value_w, pair_width, 1).astype(bf16)
    mid_w[2] = v_mid_ref[...].astype(f32).T.astype(bf16)
    unit = lax.broadcasted_iota(jnp.int32, (16, LANES), 1)
    pick = lax.broadcasted_iota(jnp.int32, (16, LANES), 0)
    first_w[4 * hidden : 4 * hidden + 16, :] = jnp.where(
        (unit == pick + (pair_width + states_width)) & (pick < 2), 1.0, 0.0
    ).astype(bf16)
    wide[0:2, :] = q_out_ref[...].astype(f32)
    wide[2:3, :] = v_out_ref[...].astype(f32).reshape(1, hidden)
    columns = wide[0:8, :].T
    for head in range(3):
        out_w[head] = jnp.broadcast_to(columns[:, head : head + 1], (hidden, 128))

    def send(part, number):
        _, mask, start, count = pieces[part][number]
        return pltpu.make_async_remote_copy(
            src_ref=table.at[part, pl.ds(0, count)],
            dst_ref=table.at[part, pl.ds(start, count)],
            send_sem=send_sem.at[part, number],
            recv_sem=recv_sem.at[part, number],
            device_id=partner(mask),
            device_id_type=MESH,
        )

    def hand_over(part, number):
        start, count = (0, 1) if number < 0 else pieces[part][number][2:]
        return pltpu.make_async_remote_copy(
            src_ref=table.at[part, pl.ds(start, count)],
            dst_ref=table.at[part, pl.ds(half + start, count)],
            send_sem=pass_send_sem.at[part, number + 1],
            recv_sem=pass_recv_sem.at[part, number + 1],
            device_id=partner(1 << plan[part][1]),
            device_id_type=MESH,
        )

    def evaluate(part):
        blocks = []
        for g in range(groups):
            start = part * part_rows + g * LANES
            block = rows_v[start : start + LANES, :]
            ones = lax.dot_general(
                first_w[...], block, (((1,), (1,)), ((), ())), preferred_element_type=f32
            )
            outs = []
            for head in range(4):
                h1 = jnp.maximum(ones[head * hidden : (head + 1) * hidden], 0.0).astype(bf16)
                kind = min(head, 2)
                h2 = jnp.maximum(
                    jnp.dot(mid_w[kind], h1, preferred_element_type=f32), 0.0
                )
                weight = out_w[kind]
                outs.append(
                    jnp.concatenate(
                        [
                            jnp.sum(h2[:, n : n + 128] * weight, axis=0, keepdims=True)
                            for n in range(0, LANES, 128)
                        ],
                        axis=1,
                    )
                )
            reward = ones[4 * hidden : 4 * hidden + 1]
            discount = ones[4 * hidden + 1 : 4 * hidden + 2]
            q_first, q_second, value_now, value_next = outs
            targets = reward + discount * value_next
            q_loss = (q_first - targets) ** 2 + (q_second - targets) ** 2
            gap = jnp.minimum(q_first, q_second) - value_now
            value_loss = jnp.where(gap < 0.0, 0.3, 0.7) * gap * gap
            blocks += [
                q_first,
                q_second,
                value_now,
                value_next,
                targets,
                q_loss,
                value_loss,
                jnp.zeros_like(q_loss),
            ]
        table[part, 0] = jnp.concatenate(blocks, axis=0).astype(bf16)

    def select(acc, part, start, count):
        def some(acc, start, count):
            piece = table[part, pl.ds(start, count)].reshape(count * groups * KINDS, LANES)
            found = jnp.dot(piece, hot[...], preferred_element_type=f32)
            where = place[part]
            for j in range(count * groups):
                acc = jnp.where(
                    where == start * groups + j, found[j * KINDS : (j + 1) * KINDS], acc
                )
            return acc

        if count <= 8:
            return some(acc, start, count)
        return lax.fori_loop(0, count // 8, lambda i, a: some(a, start + i * 8, 8), acc)

    acc = jnp.zeros((KINDS, batch), f32)

    def begin(part, stage):
        for number, piece in enumerate(pieces[part]):
            if piece[0] == stage:
                send(part, number).start()

    events = []
    for part in range(PARTS):
        for number, (stage, mask, _, _) in enumerate(pieces[part]):
            when = part * EVERY + stage * STAGE + mask.bit_count() * HOP
            events.append((when, part, number))
    events.sort()
    ready = {}

    def receive(part, number):
        send(part, number).wait_recv()
        stage = pieces[part][number][0]
        ready[part, stage] = ready.get((part, stage), 0) + 1
        if ready[part, stage] == sum(piece[0] == stage for piece in pieces[part]):
            begin(part, stage + 1)
        if plan[part][1] is not None:
            hand_over(part, number).start()

    taken = []
    late = []
    for part in range(PARTS):
        load(part).wait()
        evaluate(part)
        if part == 0:
            pl.semaphore_wait(barrier, len(partners))
        begin(part, 0)
        if plan[part][1] is not None:
            hand_over(part, -1).start()
            late.append((part, -1))
        while events and events[0][0] < (part - 1) * EVERY:
            _, p, n = events.pop(0)
            receive(p, n)
            taken.append((p, n))
    for fetch in fetches[6:]:
        fetch.wait()
    wanted = row_ref[...]
    relative = owner_ref[...] ^ me
    low = wanted & (LANES - 1)
    group = wanted // LANES
    hot[...] = jnp.where(
        lax.broadcasted_iota(jnp.int32, (LANES, batch), 0) == low, 1.0, 0.0
    ).astype(bf16)
    for part in range(PARTS):
        slot = jnp.zeros_like(relative)
        stages, last = plan[part]
        bits = [bit for stage in stages for bit in stage]
        for position, bit in enumerate(bits + ([] if last is None else [last])):
            slot = slot + (((relative >> bit) & 1) << position)
        here = (group // groups) == part
        index = jnp.where(here, slot * groups + (group - part * groups), -1)
        place[part] = jnp.broadcast_to(index, (KINDS, batch))

    for part in range(PARTS):
        acc = select(acc, part, 0, 1)
    for p, n in taken:
        acc = select(acc, p, *pieces[p][n][2:])
        if plan[p][1] is not None:
            late.append((p, n))

    def finish(acc, part, number):
        hand_over(part, number).wait_recv()
        start, count = (0, 1) if number < 0 else pieces[part][number][2:]
        return select(acc, part, half + start, count)

    for _, p, n in events:
        receive(p, n)
        acc = select(acc, p, *pieces[p][n][2:])
        if plan[p][1] is not None:
            late.append((p, n))
        if len(late) > BEHIND:
            acc = finish(acc, *late.pop(0))
    for p, n in late:
        acc = finish(acc, p, n)
    result_ref[...] = acc
    for part in range(PARTS):
        for number in range(len(pieces[part])):
            send(part, number).wait_send()
        if plan[part][1] is not None:
            for number in range(-1, len(pieces[part])):
                hand_over(part, number).wait_send()


def spread(result_ref, q_values_ref, values_ref, targets_ref, q_loss_ref, value_loss_ref):
    q_values_ref[...] = result_ref[0:2]
    values_ref[...] = result_ref[2:4]
    targets_ref[...] = result_ref[4:5]
    q_loss_ref[...] = result_ref[5:6]
    value_loss_ref[...] = result_ref[6:7]


def body(buffer, owner, local_row, q_in, q_mid, q_out, v_in, v_mid, v_out):
    dp_size, mp_size = lax.axis_size("dp"), lax.axis_size("mp")
    owners = dp_size * mp_size
    batch = local_row.shape[0]
    rows_dev, width = buffer.shape
    hidden = v_mid.shape[0]
    assert width == LANES and hidden == LANES
    groups = rows_dev // PARTS // LANES
    sends = max(len(pieces_of(stages)[0]) for stages, _ in plan_of(dp_size, mp_size))
    f32, bf16 = jnp.float32, jnp.bfloat16
    vmem = pl.BlockSpec(memory_space=pltpu.VMEM)
    hbm = pl.BlockSpec(memory_space=pltpu.HBM)
    result = pl.pallas_call(
        functools.partial(kernel, dp_size, mp_size),
        out_shape=pltpu.VMEM((KINDS, batch), f32),
        in_specs=[hbm] * 9,
        out_specs=vmem,
        scratch_shapes=[
            pltpu.VMEM((1, batch), jnp.int32),
            pltpu.VMEM((1, batch), jnp.int32),
            pltpu.VMEM((q_in.shape[1], 2, hidden), bf16),
            pltpu.VMEM(q_mid.shape, bf16),
            pltpu.VMEM(q_out.shape, bf16),
            pltpu.VMEM(v_in.shape, bf16),
            pltpu.VMEM(v_mid.shape, bf16),
            pltpu.VMEM(v_out.shape, bf16),
            pltpu.VMEM((rows_dev, width), bf16),
            pltpu.VMEM((width, hidden), f32),
            pltpu.VMEM((4 * hidden + 16, width), bf16),
            pltpu.VMEM((3, hidden, hidden), bf16),
            pltpu.VMEM((3, hidden, 128), f32),
            pltpu.VMEM((PARTS, owners, groups * KINDS, LANES), bf16),
            pltpu.VMEM((LANES, batch), bf16),
            pltpu.VMEM((PARTS, KINDS, batch), jnp.int32),
            pltpu.SemaphoreType.DMA((PARTS,)),
            pltpu.SemaphoreType.DMA((8,)),
            pltpu.SemaphoreType.DMA((PARTS, sends)),
            pltpu.SemaphoreType.DMA((PARTS, sends)),
            pltpu.SemaphoreType.DMA((PARTS, sends + 1)),
            pltpu.SemaphoreType.DMA((PARTS, sends + 1)),
        ],
        compiler_params=pltpu.CompilerParams(
            collective_id=0, has_side_effects=True, vmem_limit_bytes=48 << 20
        ),
        name="critic_exchange",
    )(
        *(
            pltpu.with_memory_space_constraint(x, pltpu.HBM)
            for x in (
                buffer,
                owner.reshape(1, batch),
                local_row.reshape(1, batch),
                jnp.transpose(q_in, (1, 0, 2)),
                q_mid,
                q_out,
                v_in,
                v_mid,
                v_out,
            )
        )
    )
    one = jax.ShapeDtypeStruct((1, batch), f32)
    two = jax.ShapeDtypeStruct((2, batch), f32)
    outs = pl.pallas_call(
        spread,
        out_shape=(two, two, one, one, one),
        in_specs=[vmem],
        out_specs=(vmem,) * 5,
        compiler_params=pltpu.CompilerParams(vmem_limit_bytes=1 << 20),
        name="spread",
    )(result)
    q_values, values, targets, q_loss, value_loss = outs
    return (
        q_values,
        values,
        targets.reshape(batch),
        q_loss.reshape(batch),
        value_loss.reshape(batch),
    )


def solution(mesh):
    return jax.shard_map(
        body,
        mesh=mesh,
        in_specs=(
            P(("dp", "mp"), None),
            P(("dp", "mp"), None),
            P(("dp", "mp")),
            P(),
            P(),
            P(),
            P(),
            P(),
            P(),
        ),
        out_specs=(
            P(None, ("dp", "mp")),
            P(None, ("dp", "mp")),
            P(("dp", "mp")),
            P(("dp", "mp")),
            P(("dp", "mp")),
        ),
        check_vma=False,
    )
```
